256 devices in a mesh: mic: 64 (over x, z_hi, y), proj: 4 (over z_lo, core).
Axes of the slice: x: 4, y: 4, z: 8 (z_hi: 4, z_lo: 2; z = z_hi * 2 + z_lo), core: 2. Of those that a mesh axis runs over, the one named last changes fastest.
Arguments:
- map_slabs: bfloat16 [20, 8, 256, 256], P('proj'), may hold values from -1.25 to 1.25
- slot_slab: int32 [20], P('proj'), may hold values from -1 to 11, as said below
- orient_index: int32 [4], replicated, may hold values from 0 to 255
- slab_lo: int32 [4], replicated, may hold values from 0 to 4
- slab_hi: int32 [4], replicated, may hold values from 8 to 12
- tile_spectrum: bfloat16 [256, 512, 1024], P(('mic', 'proj')), may hold values from -6 to 6
- prev_max: float32 [256, 512, 512], P(('mic', 'proj')), may hold values from -6 to 6
- prev_sum: float32 [256, 512, 512], P(('mic', 'proj')), may hold values from -12 to 12
- prev_sumsq: float32 [256, 512, 512], P(('mic', 'proj')), may hold values from 0.5 to 4
Outputs:
- best_score: float32 [256, 512, 512], P(('mic', 'proj'))
- score_sum: float32 [256, 512, 512], P(('mic', 'proj'))
- score_sumsq: float32 [256, 512, 512], P(('mic', 'proj'))
The draws below stay inside these ranges and needn't reach their ends.
Inputs may be any that keep to these rules, and one draw needn't show every extreme that they name: `slot_slab`: each slab 0 to 11 stands in exactly one slot; every other slot holds -1. One index of proj holds 5 slabs; the others may hold fewer, and may hold none.
All inputs are finite; a program needn't handle non-finite values.
Results may differ from the reference program's by a relative error of at most 0.0057.
Values may be sent and summed in bfloat16 or wider, within the bound.
A program may use at most 128 MiB of HBM per device.

```python
import math
import jax
import jax.numpy as jnp
from jax import lax

BOX = 256
TILE = 512
SLAB_Z = 8
SLABS = 12
SLOTS_DEV = 5
ORI = 4
NORI = 256
SLOTS = 20
TILES = 256


def draw_slot_slab(key, part):
    key_heavy = jax.random.fold_in(key, 11)
    key_order = jax.random.fold_in(key, 12)
    key_slabs = jax.random.fold_in(key, 13)
    owner_count = SLOTS // SLOTS_DEV
    heavy = jax.random.randint(key_heavy, (), 0, owner_count)
    owners = jnp.arange(SLOTS, dtype=jnp.int32) // SLOTS_DEV
    shuffled = jax.random.permutation(key_order, SLOTS).astype(jnp.int32)
    ranking = jnp.where(owners == heavy, -1 - jnp.arange(SLOTS, dtype=jnp.int32), shuffled)
    ordering = jnp.argsort(ranking, stable=True)
    chosen = ordering[:SLABS]
    slab_ids = jax.random.permutation(key_slabs, SLABS).astype(jnp.int32)
    return jnp.full((SLOTS,), -1, jnp.int32).at[chosen].set(slab_ids)


def place_ends(array, rng, least, high):
    place = [jax.random.randint(jax.random.fold_in(rng, axis), (), 0, length) for axis, length in enumerate(array.shape)]
    main_axis = array.shape.index(max(array.shape))
    neighbour = place[:main_axis] + [(place[main_axis] + 1) % array.shape[main_axis]] + place[main_axis + 1:]
    return array.at[tuple(place)].set(least).at[tuple(neighbour)].set(high)


def level_of(key, dims, pieces, low, largest):
    def one(dim, parts):
        steps = jax.random.uniform(jax.random.fold_in(jax.random.fold_in(key, 6), dim), (parts,), jnp.float32, low / len(pieces), largest / len(pieces))
        return jnp.repeat(jnp.exp(steps), dims[dim] // parts).reshape((-1,) + (1,) * (len(dims) - dim - 1))

    factor_of = one(*pieces[0])
    for cut in pieces[1:]:
        factor_of = factor_of * one(*cut)
    return factor_of


def gaussian(rng, dims, spread, limit, shards=(), kind=jnp.bfloat16):
    array = jax.random.normal(rng, dims, jnp.float32) * spread
    if len(shards) > 0:
        array = level_of(rng, dims, shards, -0.22, 0.18) * array
    return jnp.clip(array, min=-limit, max=limit).astype(kind)


def setup_inputs(seed: int = 0) -> dict:
    splits = jax.random.split(jax.random.key(seed), 10)
    map_slabs = gaussian(splits[0], (SLOTS, SLAB_Z, BOX, BOX), (2 / (SLABS * SLAB_Z) ** 0.5), 1.25, ((0, 4),))
    slot_slab = draw_slot_slab(jax.random.fold_in(splits[9], 71), 0)
    orient_index = place_ends(jax.random.randint(splits[2], (ORI,), 0, NORI), jax.random.fold_in(splits[2], 1), 0, NORI - 1).astype(jnp.int32)
    slab_lo = place_ends(jax.random.randint(splits[3], (ORI,), 0, SLABS // 3 + 1), jax.random.fold_in(splits[3], 1), 0, (SLABS // 3 + 1) - 1).astype(jnp.int32)
    slab_hi = place_ends(jax.random.randint(splits[4], (ORI,), 2 * SLABS // 3, SLABS + 1), jax.random.fold_in(splits[4], 1), 2 * SLABS // 3, SLABS).astype(jnp.int32)
    tile_spectrum = gaussian(splits[5], (TILES, TILE, 2 * TILE), 1.0, 6.0, ((0, 256),))
    prev_max = gaussian(splits[6], (TILES, TILE, TILE), 1.0, 6.0, ((0, 256),), jnp.float32)
    prev_sum = gaussian(splits[7], (TILES, TILE, TILE), 2.0, 12.0, ((0, 256),), jnp.float32)
    prev_sumsq = jnp.clip(0.5 + 3.5 * jax.random.uniform(splits[8], (TILES, TILE, TILE), jnp.float32) ** level_of(splits[8], (TILES, TILE, TILE), ((0, 256),), -0.2, 0.2), 0.5, 4.0)
    return dict(map_slabs=map_slabs, slot_slab=slot_slab, orient_index=orient_index, slab_lo=slab_lo, slab_hi=slab_hi, tile_spectrum=tile_spectrum, prev_max=prev_max, prev_sum=prev_sum, prev_sumsq=prev_sumsq)


max_slope = 0.5
golden_angle = 2.399963

def rounded(value):
    return lax.optimization_barrier(value.astype(jnp.bfloat16)).astype(jnp.float32)

def matmul(left_op, right_op):
    return jnp.dot(left_op.astype(jnp.float32), right_op.astype(jnp.float32), precision=lax.Precision.HIGHEST)

def tent_weight(offsets):
    return jnp.maximum(0.0, 1.0 - jnp.abs(offsets))

def orient_slopes(orient_index):
    search_step = orient_index.astype(jnp.float32)
    radius = max_slope * jnp.sqrt((search_step + 0.5) / NORI)
    return (radius * jnp.cos(golden_angle * search_step), radius * jnp.sin(golden_angle * search_step))

def phase_parts(freq_count, pixel_count, length):
    freqs = jnp.arange(freq_count, dtype=jnp.int32)[:, None]
    pixels = jnp.arange(pixel_count, dtype=jnp.int32)[None, :]
    turn_frac = (freqs * pixels % length).astype(jnp.float32) / length
    norm_scale = 1.0 / math.sqrt(length)
    return (jnp.cos(2.0 * math.pi * turn_frac) * norm_scale, jnp.sin(2.0 * math.pi * turn_frac) * norm_scale)

def dft_tables(box_edge, tile_edge):
    row_cos, row_sin = phase_parts(box_edge, tile_edge, tile_edge)
    row_table = rounded(jnp.concatenate([row_cos, -row_sin], axis=1))
    col_cos, col_sin = phase_parts(tile_edge, box_edge, tile_edge)
    column_table = rounded(jnp.concatenate([col_cos, -col_sin], axis=0))
    full_cos, full_sin = phase_parts(tile_edge, tile_edge, tile_edge)
    inverse_table = rounded(jnp.concatenate([full_cos, full_sin], axis=1))
    final_table = rounded(jnp.concatenate([full_cos, -full_sin], axis=1))
    return (row_table, column_table, inverse_table, final_table)

def correlate(row_block, spectrum_tile, column_table, inverse_table, final_table):
    edge = spectrum_tile.shape[0]
    stacked = matmul(column_table, row_block)
    real_part = stacked[:edge, :edge] - stacked[edge:, edge:]
    imag_part = stacked[:edge, edge:] + stacked[edge:, :edge]
    micro_real = spectrum_tile[:, :edge].astype(jnp.float32)
    micro_imag = spectrum_tile[:, edge:].astype(jnp.float32)
    product = rounded(jnp.concatenate([micro_real * real_part + micro_imag * imag_part, micro_imag * real_part - micro_real * imag_part], axis=0))
    halfway = matmul(product, inverse_table)
    half_real = halfway[:edge, :edge] - halfway[edge:, edge:]
    half_imag = halfway[:edge, edge:] + halfway[edge:, :edge]
    half_stack = rounded(jnp.concatenate([half_real, half_imag], axis=0))
    return matmul(final_table, half_stack)

def reference(map_slabs, slot_slab, orient_index, slab_lo, slab_hi, tile_spectrum, prev_max, prev_sum, prev_sumsq):
    slope_x, slope_y = orient_slopes(orient_index)
    center = (SLABS * SLAB_Z - 1) / 2.0
    positions = jnp.arange(BOX, dtype=jnp.int32).astype(jnp.float32)
    within = jnp.arange(SLAB_Z, dtype=jnp.int32)
    projection = jnp.zeros((ORI, BOX, BOX), jnp.float32)
    for slot_number in range(SLOTS):
        slab_id = slot_slab[slot_number]
        depths = (slab_id * SLAB_Z + within).astype(jnp.float32) - center
        shift_x = slope_x[:, None] * depths[None, :]
        shift_y = slope_y[:, None] * depths[None, :]
        left_tent = rounded(tent_weight(positions[None, None, None, :] - positions[None, None, :, None] - shift_x[:, :, None, None]))
        right_tent = rounded(tent_weight(positions[None, None, None, :] - positions[None, None, :, None] - shift_y[:, :, None, None]))
        slab_map = map_slabs[slot_number].astype(jnp.float32)
        sheared = rounded(jnp.einsum('ojax,jxy->ojay', left_tent, slab_map, precision=lax.Precision.HIGHEST))
        slab_term = jnp.einsum('ojay,ojby->oab', sheared, right_tent, precision=lax.Precision.HIGHEST)
        inside = ((slab_id >= slab_lo) & (slab_id < slab_hi)).astype(jnp.float32)
        projection = projection + inside[:, None, None] * slab_term
    template = rounded(projection)
    row_table, column_table, inverse_table, final_table = dft_tables(BOX, TILE)
    row_spectrum = rounded(jnp.einsum('oay,yk->oak', template, row_table, precision=lax.Precision.HIGHEST))

    def per_tile(operands):
        spectrum_tile, best_seen, totals, squares = operands

        def per_orient(orient, running):
            best_run, total_run, square_run = running
            scores = correlate(row_spectrum[orient], spectrum_tile, column_table, inverse_table, final_table)
            return (jnp.maximum(best_run, scores), total_run + scores, square_run + scores * scores)
        return lax.fori_loop(0, ORI, per_orient, (best_seen, totals, squares))
    best_score, score_sum, score_sumsq = lax.map(per_tile, (tile_spectrum, prev_max, prev_sum, prev_sumsq))
    return (best_score, score_sum, score_sumsq)
```

```python
import functools
import math

import jax
import jax.numpy as jnp
import ml_dtypes
import numpy as np
from jax import lax
from jax.experimental import pallas as pl
from jax.experimental.pallas import tpu as pltpu
from jax.sharding import PartitionSpec as P

MESH = pl.DeviceIdType.MESH
SLAB_Z = 8
SLABS = 12
NORI = 256
BOX = 256
TILE = 512
ORI = 4
SLOTS = 5
HALF = BOX // 2
ROWS = 272
GOLDEN = 2.399963
MAX_SLOPE = 0.5


def turns(freqs, pixels):
    angle = 2.0 * np.pi * ((freqs[:, None] * pixels[None, :]) % TILE) / TILE
    return np.cos(angle) / math.sqrt(TILE), np.sin(angle) / math.sqrt(TILE)


def bf16(array):
    return np.asarray(array, np.float32).astype(ml_dtypes.bfloat16)


@functools.lru_cache(maxsize=None)
def tables():
    evens, odds = np.arange(0, BOX, 2), np.arange(1, BOX, 2)
    freq = np.concatenate([evens, odds])
    all_freq = np.concatenate([freq, [BOX]])
    cos, sin = turns(all_freq, np.arange(BOX))
    column = np.zeros((2 * ROWS, BOX))
    column[: BOX + 1] = cos
    column[ROWS : ROWS + BOX + 1] = -sin
    spread = []
    for pixels in (evens, odds):
        parts = []
        for freqs in (evens, odds):
            cos, sin = turns(pixels, freqs)
            parts.append(np.block([[cos, -sin], [sin, cos]]))
        spread.append(np.concatenate(parts, axis=1))
    inverse = []
    for freqs in (evens, odds):
        cos, sin = turns(np.concatenate([freqs, freqs + BOX]), np.arange(BOX))
        inverse.append(np.block([[cos, sin], [-sin, cos]]))
    final = []
    for freqs in (evens, odds):
        cos, sin = turns(np.arange(BOX), freqs)
        final.append(np.concatenate([cos, -sin], axis=1))
    final[0][:, 0] *= 0.5
    final[0][:, HALF] = 0.5 * turns(np.arange(BOX), np.array([BOX]))[0][:, 0]
    return tuple(
        bf16(t)
        for t in (
            column,
            np.stack(spread),
            np.stack(inverse),
            np.stack(final),
        )
    )


def dot(a, b):
    return jnp.dot(a, b, preferred_element_type=jnp.float32)


def fill_selections(rowsel, colsel):
    one_hot = lambda mask: jnp.where(mask, 1.0, 0.0).astype(jnp.bfloat16)
    lane = lax.broadcasted_iota(jnp.int32, (ROWS, 128), 1)
    row = lax.broadcasted_iota(jnp.int32, (ROWS, 128), 0)
    freq = jnp.where(row < 128, 2 * row, jnp.where(row <= BOX, 2 * row - 255, -1))
    freq = jnp.where(row == BOX, BOX, freq)
    mirror = jnp.where(freq <= 0, freq, TILE - freq)
    for block in range(4):
        lanes = slice(block * 128, (block + 1) * 128)
        rowsel[:ROWS, lanes] = one_hot(lane + block * 128 == freq)
        rowsel[ROWS:, lanes] = one_hot(lane + block * 128 == mirror)
    twice = 2 * lax.broadcasted_iota(jnp.int32, (TILE, 128), 1)
    source = lax.broadcasted_iota(jnp.int32, (TILE, 128), 0)
    for block, offset in enumerate((0, 1, BOX, BOX + 1)):
        lanes = slice(block * 128, (block + 1) * 128)
        colsel[:TILE, lanes] = one_hot(source - twice == offset)
        colsel[TILE:, lanes] = one_hot((source + twice + offset) % TILE == 0)


def project_kernel(
    orient_ref,
    slot_ref,
    lo_ref,
    hi_ref,
    map_ref,
    tile_ref,
    template_ref,
    folded_ref,
    slabs,
    tile,
    rowsel,
    colsel,
    left,
    right,
    sheared,
    acc,
    sib_recv,
    z_send,
    z_recv,
    template,
    picked,
    folded,
    in_sem,
    slab_sem,
    out_sem,
    send_sem,
    recv_sem,
):
    mic, proj = lax.axis_index("mic"), lax.axis_index("proj")
    x, z_hi, y = mic // 16, (mic // 4) % 4, mic % 4
    z_lo, core = proj // 2, proj % 2
    own = (x + y) % 4

    def device(dx, dy, which_z, which_core):
        chip = (((x + dx + 4) % 4) * 4 + z_hi) * 4 + (y + dy + 4) % 4
        return (chip, which_z * 2 + which_core)

    sibling = device(0, 0, z_lo, 1 - core)
    across = device(0, 0, 1 - z_lo, core)
    along = [(1 - core, core), (core - 1, -core), (1 - 2 * core, 1 - 2 * core)]
    targets = [device(dx, dy, z_lo, c) for dx, dy in along for c in (0, 1)]
    sources = [
        device(1, 0, z_lo, 0),
        device(-1, 0, z_lo, 0),
        device(-1, -1, z_lo, 0),
        device(0, 1, z_lo, 1),
        device(0, -1, z_lo, 1),
        device(1, 1, z_lo, 1),
    ]

    barrier = pltpu.get_barrier_semaphore()
    for peer in [sibling, across] + sources:
        pl.semaphore_signal(barrier, inc=1, device_id=peer, device_id_type=MESH)

    for slot in range(SLOTS):
        pltpu.make_async_copy(map_ref.at[slot], slabs.at[slot], slab_sem.at[slot]).start()
    loads = [
        pltpu.make_async_copy(src, dst, in_sem.at[i])
        for i, (src, dst) in enumerate(((tile_ref.at[0], tile),))
    ]
    for load in loads:
        load.start()

    fill_selections(rowsel, colsel)

    step = jnp.full((SLAB_Z, 128), orient_ref[own]).astype(jnp.float32)
    radius = MAX_SLOPE * jnp.sqrt((step + 0.5) / NORI)
    slope_x = radius * jnp.cos(GOLDEN * step)
    slope_y = radius * jnp.sin(GOLDEN * step)
    within = lax.broadcasted_iota(jnp.int32, (SLAB_Z, 128), 0)
    center = (SLABS * SLAB_Z - 1) / 2.0

    def taps(shift, weight):
        low = jnp.floor(shift)
        first = jnp.maximum(0.0, 1.0 - jnp.abs(low - shift)) * weight
        second = jnp.maximum(0.0, 1.0 - jnp.abs((low + 1.0) - shift)) * weight
        return low, first, second

    left_gap = (
        lax.broadcasted_iota(jnp.int32, (160, 128), 1) - lax.broadcasted_iota(jnp.int32, (160, 128), 0)
    ).astype(jnp.float32).astype(jnp.bfloat16)
    right_gap = (
        lax.broadcasted_iota(jnp.int32, (BOX, 128), 0) - 2 * lax.broadcasted_iota(jnp.int32, (BOX, 128), 1)
    ).astype(jnp.float32).astype(jnp.bfloat16)
    zero = jnp.zeros((), jnp.bfloat16)
    for j in range(SLAB_Z):
        left[j, 160:, :128] = jnp.zeros((96, 128), jnp.bfloat16)
        left[j, :96, 128:] = jnp.zeros((96, 128), jnp.bfloat16)
    acc[...] = jnp.zeros_like(acc)

    def one_slot(slot, carry):
        slab = jnp.full((SLAB_Z, 128), slot_ref[slot])
        depth = (slab * SLAB_Z + within).astype(jnp.float32) - center
        inside = jnp.where((slab >= lo_ref[own]) & (slab < hi_ref[own]), 1.0, 0.0)
        nx, x0, x1 = taps(slope_x * depth, inside)
        ny, y0, y1 = taps(slope_y * depth, 1.0)
        for j in range(SLAB_Z):
            row = lambda v, shape: jnp.broadcast_to(v[j : j + 1].astype(jnp.bfloat16), shape)
            w0, w1 = row(x0, (160, 128)), row(x1, (160, 128))
            for first, lanes, offset in ((0, 0, 0.0), (96, 128, 32.0)):
                block = jnp.where(
                    left_gap == row(nx - offset, (160, 128)),
                    w0,
                    jnp.where(left_gap == row(nx + 1.0 - offset, (160, 128)), w1, zero),
                )
                left[j, first : first + 160, lanes : lanes + 128] = block
            w0, w1 = row(y0, (BOX, 128)), row(y1, (BOX, 128))
            at0, at1, at2 = (right_gap == row(ny + k, (BOX, 128)) for k in (0.0, 1.0, 2.0))
            right[j * BOX : (j + 1) * BOX, :128] = jnp.where(at0, w0, jnp.where(at1, w1, zero))
            right[j * BOX : (j + 1) * BOX, 128:] = jnp.where(at1, w0, jnp.where(at2, w1, zero))
        pltpu.make_async_copy(map_ref.at[slot], slabs.at[slot], slab_sem.at[slot]).wait()
        for j in range(SLAB_Z):
            sheared[:, j * BOX : (j + 1) * BOX] = dot(left[j], slabs[slot, j]).astype(jnp.bfloat16)
        acc[...] += dot(sheared[...], right[...])
        return carry

    lax.fori_loop(0, SLOTS, one_slot, 0)

    def send(i, arrival, src, dst, peer):
        return pltpu.make_async_remote_copy(
            src_ref=src,
            dst_ref=dst,
            send_sem=send_sem.at[i],
            recv_sem=recv_sem.at[arrival],
            device_id=peer,
            device_id_type=MESH,
        )

    mine = pl.ds(pl.multiple_of(core * HALF, HALF), HALF)
    theirs = pl.ds(pl.multiple_of((1 - core) * HALF, HALF), HALF)
    pl.semaphore_wait(barrier, 8)
    hop = send(0, 0, acc.at[theirs], sib_recv, sibling)
    hop.start()
    for load in loads:
        load.wait()
    rows = dot(rowsel[...], tile[...])
    picked[:ROWS, :TILE] = rows[:ROWS, :TILE].astype(jnp.bfloat16)
    picked[:ROWS, TILE:] = rows[ROWS:, :TILE].astype(jnp.bfloat16)
    picked[ROWS:, :TILE] = rows[:ROWS, TILE:].astype(jnp.bfloat16)
    picked[ROWS:, TILE:] = (-rows[ROWS:, TILE:]).astype(jnp.bfloat16)
    hop.wait()
    chip_sum = acc[mine, :] + sib_recv[...]
    z_send[...] = chip_sum.astype(jnp.bfloat16)
    hop = send(1, 1, z_send, z_recv, across)
    hop.start()
    folded[...] = dot(picked[...], colsel[...])
    save = pltpu.make_async_copy(folded, folded_ref, out_sem.at[0])
    save.start()
    hop.wait()
    template[own, mine, :] = (chip_sum + z_recv[...].astype(jnp.float32)).astype(jnp.bfloat16)
    block = template.at[own, mine]
    hops = [send(3 + i, 3 + core * 3 + i // 2, block, block, peer) for i, peer in enumerate(targets)]
    hops.append(send(2, 2, block, block, sibling))
    for hop in hops:
        hop.start()
    arrivals = [(2, own, 1 - core)]
    for source_core in range(2):
        for i, offset in enumerate((3, 1, 2)):
            arrivals.append((3 + source_core * 3 + i, (own + offset) % 4, source_core))
    for arrival, orient, source_core in arrivals:
        landed = template.at[orient, pl.ds(pl.multiple_of(source_core * HALF, HALF), HALF)]
        send(2, arrival, landed, landed, sibling).wait_recv()
    for hop in hops:
        hop.wait_send()
    out = pltpu.make_async_copy(template, template_ref, out_sem.at[1])
    out.start()
    out.wait()
    save.wait()


def correlate_kernel(
    template_ref,
    folded_ref,
    column_ref,
    spread_ref,
    inverse_ref,
    final_ref,
    max_ref,
    sum_ref,
    sumsq_ref,
    out_max_ref,
    out_sum_ref,
    out_sumsq_ref,
    template,
    folded,
    column,
    spread,
    inverse,
    final,
    best,
    total,
    square,
    cs,
    prod,
    half,
    even_part,
    odd_part,
    in_sem,
    out_sem,
):
    copies = [
        pltpu.make_async_copy(src, dst, in_sem.at[i])
        for i, (src, dst) in enumerate(
            (
                (template_ref, template),
                (column_ref, column),
                (spread_ref, spread),
                (folded_ref, folded),
                (inverse_ref, inverse),
                (final_ref, final),
                (max_ref.at[0], best),
                (sum_ref.at[0], total),
                (sumsq_ref.at[0], square),
            )
        )
    ]
    for copy in copies:
        copy.start()
    copies[0].wait()
    copies[1].wait()
    for o in range(ORI):
        value = dot(column[...], template[o]).astype(jnp.bfloat16)
        cs[o, :, 0:128] = value[:ROWS, :128]
        cs[o, :, 128:256] = value[ROWS:, :128]
        cs[o, :, 256:384] = value[:ROWS, 128:]
        cs[o, :, 384:512] = value[ROWS:, 128:]
    copies[2].wait()
    copies[3].wait()
    for o in range(ORI):
        for q in range(2):
            even = dot(cs[o, :, :256], spread[0, :, q * 256 : (q + 1) * 256])
            odd = dot(cs[o, :, 256:], spread[1, :, q * 256 : (q + 1) * 256])
            for h, spec in enumerate((even + odd, even - odd)):
                lanes = slice((2 * h + q) * 128, (2 * h + q + 1) * 128)
                t_re, t_im = folded[:ROWS, lanes], folded[ROWS:, lanes]
                s_re, s_im = spec[:, :128], spec[:, 128:]
                re = t_re * s_re + t_im * s_im
                im = t_im * s_re - t_re * s_im
                prod[o, q, 8:, h * 128 : (h + 1) * 128] = re[8:BOX].astype(jnp.bfloat16)
                prod[o, q, 8:, 256 + h * 128 : 256 + (h + 1) * 128] = im[8:BOX].astype(jnp.bfloat16)
                top_re = re[:8] - im[BOX : BOX + 8]
                top_im = im[:8] + re[BOX : BOX + 8]
                prod[o, q, :8, h * 128 : (h + 1) * 128] = top_re.astype(jnp.bfloat16)
                prod[o, q, :8, 256 + h * 128 : 256 + (h + 1) * 128] = top_im.astype(jnp.bfloat16)
    copies[4].wait()
    for o in range(ORI):
        even = dot(prod[o, 0], inverse[0])
        odd = dot(prod[o, 1], inverse[1])
        low, high = (even + odd).astype(jnp.bfloat16), (even - odd).astype(jnp.bfloat16)
        for parity in range(2):
            rows = slice(parity * 128, (parity + 1) * 128)
            half[o, parity, :128, :256] = low[rows, :256]
            half[o, parity, 128:, :256] = low[rows, 256:]
            half[o, parity, :128, 256:] = high[rows, :256]
            half[o, parity, 128:, 256:] = high[rows, 256:]
    for copy in copies[5:]:
        copy.wait()
    outs = []
    for block in range(2):
        lanes = slice(block * 256, (block + 1) * 256)
        for o in range(ORI):
            even_part[o] = dot(final[0], half[o, 0, :, lanes])
            odd_part[o] = dot(final[1], half[o, 1, :, lanes])

        def combine(i, carry):
            rows = pl.ds(pl.multiple_of(i * 16, 16), 16)
            high_rows = pl.ds(pl.multiple_of(i * 16 + BOX, 16), 16)
            for sign, dest in ((1, rows), (-1, high_rows)):
                peak, run, energy = best[dest, lanes], total[dest, lanes], square[dest, lanes]
                for o in range(ORI):
                    even, odd = even_part[o, rows, :], odd_part[o, rows, :]
                    score = even + odd if sign == 1 else even - odd
                    peak, run, energy = jnp.maximum(peak, score), run + score, energy + score * score
                best[dest, lanes], total[dest, lanes], square[dest, lanes] = peak, run, energy
            return carry

        lax.fori_loop(0, BOX // 16, combine, 0)
        for i, (src, dst) in enumerate(((best, out_max_ref), (total, out_sum_ref), (square, out_sumsq_ref))):
            copy = pltpu.make_async_copy(src.at[:, lanes], dst.at[0, :, lanes], out_sem.at[block * 3 + i])
            copy.start()
            outs.append(copy)
    for copy in outs:
        copy.wait()


def body(map_slabs, slot_slab, orient_index, slab_lo, slab_hi, tile_spectrum, prev_max, prev_sum, prev_sumsq):
    column, spread, inverse, final = (jnp.asarray(t) for t in tables())
    smem = pl.BlockSpec(memory_space=pltpu.SMEM)
    hbm = pl.BlockSpec(memory_space=pl.ANY)
    vmem = pltpu.VMEM
    template, folded = pl.pallas_call(
        project_kernel,
        name="project",
        out_shape=(
            jax.ShapeDtypeStruct((ORI, BOX, BOX), jnp.bfloat16),
            jax.ShapeDtypeStruct((2 * ROWS, TILE), jnp.float32),
        ),
        in_specs=[smem] * 4 + [hbm] * 2,
        out_specs=(hbm, hbm),
        scratch_shapes=[
            vmem((SLOTS, SLAB_Z, BOX, BOX), jnp.bfloat16),
            vmem((TILE, 2 * TILE), jnp.bfloat16),
            vmem((2 * ROWS, TILE), jnp.bfloat16),
            vmem((2 * TILE, TILE), jnp.bfloat16),
            vmem((SLAB_Z, BOX, BOX), jnp.bfloat16),
            vmem((SLAB_Z * BOX, BOX), jnp.bfloat16),
            vmem((BOX, SLAB_Z * BOX), jnp.bfloat16),
            vmem((BOX, BOX), jnp.float32),
            vmem((HALF, BOX), jnp.float32),
            vmem((HALF, BOX), jnp.bfloat16),
            vmem((HALF, BOX), jnp.bfloat16),
            vmem((ORI, BOX, BOX), jnp.bfloat16),
            vmem((2 * ROWS, 2 * TILE), jnp.bfloat16),
            vmem((2 * ROWS, TILE), jnp.float32),
            pltpu.SemaphoreType.DMA((1,)),
            pltpu.SemaphoreType.DMA((SLOTS,)),
            pltpu.SemaphoreType.DMA((2,)),
            pltpu.SemaphoreType.DMA((9,)),
            pltpu.SemaphoreType.DMA((9,)),
        ],
        compiler_params=pltpu.CompilerParams(
            collective_id=0, has_side_effects=True, vmem_limit_bytes=40 << 20
        ),
    )(orient_index, slot_slab, slab_lo, slab_hi, map_slabs, tile_spectrum)
    plane = jax.ShapeDtypeStruct((1, TILE, TILE), jnp.float32)
    return pl.pallas_call(
        correlate_kernel,
        name="correlate",
        out_shape=(plane, plane, plane),
        in_specs=[hbm] * 9,
        out_specs=(hbm, hbm, hbm),
        scratch_shapes=[
            vmem((ORI, BOX, BOX), jnp.bfloat16),
            vmem((2 * ROWS, TILE), jnp.float32),
            vmem((2 * ROWS, BOX), jnp.bfloat16),
            vmem((2, BOX, TILE), jnp.bfloat16),
            vmem((2, TILE, TILE), jnp.bfloat16),
            vmem((2, BOX, BOX), jnp.bfloat16),
            vmem((TILE, TILE), jnp.float32),
            vmem((TILE, TILE), jnp.float32),
            vmem((TILE, TILE), jnp.float32),
            vmem((ORI, ROWS, TILE), jnp.bfloat16),
            vmem((ORI, 2, BOX, TILE), jnp.bfloat16),
            vmem((ORI, 2, BOX, TILE), jnp.bfloat16),
            vmem((ORI, BOX, BOX), jnp.float32),
            vmem((ORI, BOX, BOX), jnp.float32),
            pltpu.SemaphoreType.DMA((9,)),
            pltpu.SemaphoreType.DMA((6,)),
        ],
        compiler_params=pltpu.CompilerParams(vmem_limit_bytes=40 << 20),
    )(template, folded, column, spread, inverse, final, prev_max, prev_sum, prev_sumsq)


def solution(mesh):
    tile_spec = P(("mic", "proj"), None, None)
    return jax.shard_map(
        body,
        mesh=mesh,
        in_specs=(P("proj", None, None, None), P("proj"), P(), P(), P(), tile_spec, tile_spec, tile_spec, tile_spec),
        out_specs=(tile_spec, tile_spec, tile_spec),
        check_vma=False,
    )
```

```python
import functools
import math

import jax
import jax.numpy as jnp
import ml_dtypes
import numpy as np
from jax import lax
from jax.experimental import pallas as pl
from jax.experimental.pallas import tpu as pltpu
from jax.sharding import PartitionSpec as P

MESH = pl.DeviceIdType.MESH
SLAB_Z = 8
SLABS = 12
NORI = 256
BOX = 256
TILE = 512
ORI = 4
SLOTS = 5
HALF = BOX // 2
ROWS = 272
GOLDEN = 2.399963
MAX_SLOPE = 0.5


def turns(freqs, pixels):
    angle = 2.0 * np.pi * ((freqs[:, None] * pixels[None, :]) % TILE) / TILE
    return np.cos(angle) / math.sqrt(TILE), np.sin(angle) / math.sqrt(TILE)


def bf16(array):
    return np.asarray(array, np.float32).astype(ml_dtypes.bfloat16)


@functools.lru_cache(maxsize=None)
def tables():
    evens, odds = np.arange(0, BOX, 2), np.arange(1, BOX, 2)
    freq = np.concatenate([evens, odds])
    all_freq = np.concatenate([freq, [BOX]])
    cos, sin = turns(all_freq, np.arange(BOX))
    column = np.zeros((2 * ROWS, BOX))
    column[: BOX + 1] = cos
    column[ROWS : ROWS + BOX + 1] = -sin
    spread = []
    for pixels in (evens, odds):
        parts = []
        for freqs in (evens, odds):
            cos, sin = turns(pixels, freqs)
            parts.append(np.block([[cos, -sin], [sin, cos]]))
        spread.append(np.concatenate(parts, axis=1))
    inverse = []
    for freqs in (evens, odds):
        cos, sin = turns(np.concatenate([freqs, freqs + BOX]), np.arange(BOX))
        inverse.append(np.block([[cos, sin], [-sin, cos]]))
    final = []
    for freqs in (evens, odds):
        cos, sin = turns(np.arange(BOX), freqs)
        final.append(np.concatenate([cos, -sin], axis=1))
    final[0][:, 0] *= 0.5
    final[0][:, HALF] = 0.5 * turns(np.arange(BOX), np.array([BOX]))[0][:, 0]
    return tuple(
        bf16(t)
        for t in (
            column,
            np.stack(spread),
            np.stack(inverse),
            np.stack(final),
        )
    )


def dot(a, b):
    return jnp.dot(a, b, preferred_element_type=jnp.float32)


def fill_selections(rowsel, colsel):
    one_hot = lambda mask: jnp.where(mask, 1.0, 0.0).astype(jnp.bfloat16)
    lane = lax.broadcasted_iota(jnp.int32, (ROWS, 128), 1)
    row = lax.broadcasted_iota(jnp.int32, (ROWS, 128), 0)
    freq = jnp.where(row < 128, 2 * row, jnp.where(row <= BOX, 2 * row - 255, -1))
    freq = jnp.where(row == BOX, BOX, freq)
    mirror = jnp.where(freq <= 0, freq, TILE - freq)
    for block in range(4):
        lanes = slice(block * 128, (block + 1) * 128)
        rowsel[:ROWS, lanes] = one_hot(lane + block * 128 == freq)
        rowsel[ROWS:, lanes] = one_hot(lane + block * 128 == mirror)
    twice = 2 * lax.broadcasted_iota(jnp.int32, (TILE, 128), 1)
    source = lax.broadcasted_iota(jnp.int32, (TILE, 128), 0)
    for block, offset in enumerate((0, 1, BOX, BOX + 1)):
        lanes = slice(block * 128, (block + 1) * 128)
        colsel[:TILE, lanes] = one_hot(source - twice == offset)
        colsel[TILE:, lanes] = one_hot((source + twice + offset) % TILE == 0)


def project_kernel(
    orient_ref,
    slot_ref,
    lo_ref,
    hi_ref,
    map_ref,
    tile_ref,
    template,
    folded,
    slabs,
    tile,
    rowsel,
    colsel,
    left,
    right,
    sheared,
    acc,
    sib_recv,
    z_send,
    z_recv,
    picked,
    in_sem,
    slab_sem,
    send_sem,
    recv_sem,
):
    mic, proj = lax.axis_index("mic"), lax.axis_index("proj")
    x, z_hi, y = mic // 16, (mic // 4) % 4, mic % 4
    z_lo, core = proj // 2, proj % 2
    own = (x + y) % 4

    def device(dx, dy, which_z, which_core):
        chip = (((x + dx + 4) % 4) * 4 + z_hi) * 4 + (y + dy + 4) % 4
        return (chip, which_z * 2 + which_core)

    sibling = device(0, 0, z_lo, 1 - core)
    across = device(0, 0, 1 - z_lo, core)
    along = [(1 - core, core), (core - 1, -core), (1 - 2 * core, 1 - 2 * core)]
    targets = [device(dx, dy, z_lo, c) for dx, dy in along for c in (0, 1)]
    sources = [
        device(1, 0, z_lo, 0),
        device(-1, 0, z_lo, 0),
        device(-1, -1, z_lo, 0),
        device(0, 1, z_lo, 1),
        device(0, -1, z_lo, 1),
        device(1, 1, z_lo, 1),
    ]

    barrier = pltpu.get_barrier_semaphore()
    for peer in [sibling, across] + sources:
        pl.semaphore_signal(barrier, inc=1, device_id=peer, device_id_type=MESH)

    for slot in range(SLOTS):
        pltpu.make_async_copy(map_ref.at[slot], slabs.at[slot], slab_sem.at[slot]).start()
    loads = [
        pltpu.make_async_copy(src, dst, in_sem.at[i])
        for i, (src, dst) in enumerate(((tile_ref.at[0], tile),))
    ]
    for load in loads:
        load.start()

    fill_selections(rowsel, colsel)

    step = jnp.full((SLAB_Z, 128), orient_ref[own]).astype(jnp.float32)
    radius = MAX_SLOPE * jnp.sqrt((step + 0.5) / NORI)
    slope_x = radius * jnp.cos(GOLDEN * step)
    slope_y = radius * jnp.sin(GOLDEN * step)
    within = lax.broadcasted_iota(jnp.int32, (SLAB_Z, 128), 0)
    center = (SLABS * SLAB_Z - 1) / 2.0

    def taps(shift, weight):
        low = jnp.floor(shift)
        first = jnp.maximum(0.0, 1.0 - jnp.abs(low - shift)) * weight
        second = jnp.maximum(0.0, 1.0 - jnp.abs((low + 1.0) - shift)) * weight
        return low, first, second

    left_gap = (
        lax.broadcasted_iota(jnp.int32, (160, 128), 1) - lax.broadcasted_iota(jnp.int32, (160, 128), 0)
    ).astype(jnp.float32).astype(jnp.bfloat16)
    right_gap = (
        lax.broadcasted_iota(jnp.int32, (BOX, 128), 0) - 2 * lax.broadcasted_iota(jnp.int32, (BOX, 128), 1)
    ).astype(jnp.float32).astype(jnp.bfloat16)
    zero = jnp.zeros((), jnp.bfloat16)
    for j in range(SLAB_Z):
        left[j, 160:, :128] = jnp.zeros((96, 128), jnp.bfloat16)
        left[j, :96, 128:] = jnp.zeros((96, 128), jnp.bfloat16)
    acc[...] = jnp.zeros_like(acc)

    def one_slot(slot, carry):
        pltpu.make_async_copy(map_ref.at[slot], slabs.at[slot], slab_sem.at[slot]).wait()
        slab = jnp.full((SLAB_Z, 128), slot_ref[slot])
        depth = (slab * SLAB_Z + within).astype(jnp.float32) - center
        inside = jnp.where((slab >= lo_ref[own]) & (slab < hi_ref[own]), 1.0, 0.0)
        nx, x0, x1 = taps(slope_x * depth, inside)
        ny, y0, y1 = taps(slope_y * depth, 1.0)
        for j in range(SLAB_Z):
            row = lambda v, shape: jnp.broadcast_to(v[j : j + 1].astype(jnp.bfloat16), shape)
            w0, w1 = row(x0, (160, 128)), row(x1, (160, 128))
            for first, lanes, offset in ((0, 0, 0.0), (96, 128, 32.0)):
                block = jnp.where(
                    left_gap == row(nx - offset, (160, 128)),
                    w0,
                    jnp.where(left_gap == row(nx + 1.0 - offset, (160, 128)), w1, zero),
                )
                left[j, first : first + 160, lanes : lanes + 128] = block
            w0, w1 = row(y0, (BOX, 128)), row(y1, (BOX, 128))
            at0, at1, at2 = (right_gap == row(ny + k, (BOX, 128)) for k in (0.0, 1.0, 2.0))
            right[j * BOX : (j + 1) * BOX, :128] = jnp.where(at0, w0, jnp.where(at1, w1, zero))
            right[j * BOX : (j + 1) * BOX, 128:] = jnp.where(at1, w0, jnp.where(at2, w1, zero))
            sheared[:, j * BOX : (j + 1) * BOX] = dot(left[j], slabs[slot, j]).astype(jnp.bfloat16)
        acc[...] += dot(sheared[...], right[...])
        return carry

    lax.fori_loop(0, SLOTS, one_slot, 0)

    def send(i, arrival, src, dst, peer):
        return pltpu.make_async_remote_copy(
            src_ref=src,
            dst_ref=dst,
            send_sem=send_sem.at[i],
            recv_sem=recv_sem.at[arrival],
            device_id=peer,
            device_id_type=MESH,
        )

    mine = pl.ds(pl.multiple_of(core * HALF, HALF), HALF)
    theirs = pl.ds(pl.multiple_of((1 - core) * HALF, HALF), HALF)
    pl.semaphore_wait(barrier, 8)
    hop = send(0, 0, acc.at[theirs], sib_recv, sibling)
    hop.start()
    for load in loads:
        load.wait()
    rows = dot(rowsel[...], tile[...])
    picked[:ROWS, :TILE] = rows[:ROWS, :TILE].astype(jnp.bfloat16)
    picked[:ROWS, TILE:] = rows[ROWS:, :TILE].astype(jnp.bfloat16)
    picked[ROWS:, :TILE] = rows[:ROWS, TILE:].astype(jnp.bfloat16)
    picked[ROWS:, TILE:] = (-rows[ROWS:, TILE:]).astype(jnp.bfloat16)
    hop.wait()
    chip_sum = acc[mine, :] + sib_recv[...]
    z_send[...] = chip_sum.astype(jnp.bfloat16)
    hop = send(1, 1, z_send, z_recv, across)
    hop.start()
    folded[...] = dot(picked[...], colsel[...])
    hop.wait()
    template[own, mine, :] = (chip_sum + z_recv[...].astype(jnp.float32)).astype(jnp.bfloat16)
    block = template.at[own, mine]
    hops = [send(3 + i, 3 + core * 3 + i // 2, block, block, peer) for i, peer in enumerate(targets)]
    hops.append(send(2, 2, block, block, sibling))
    for hop in hops:
        hop.start()
    arrivals = [(2, own, 1 - core)]
    for source_core in range(2):
        for i, offset in enumerate((3, 1, 2)):
            arrivals.append((3 + source_core * 3 + i, (own + offset) % 4, source_core))
    for arrival, orient, source_core in arrivals:
        landed = template.at[orient, pl.ds(pl.multiple_of(source_core * HALF, HALF), HALF)]
        send(2, arrival, landed, landed, sibling).wait_recv()
    for hop in hops:
        hop.wait_send()


def correlate_kernel(
    template,
    folded,
    column,
    spread,
    inverse,
    final,
    max_ref,
    sum_ref,
    sumsq_ref,
    out_max_ref,
    out_sum_ref,
    out_sumsq_ref,
    best,
    total,
    square,
    cs,
    prod,
    half,
    even_part,
    odd_part,
    out_sem,
):
    for o in range(ORI):
        value = dot(column[...], template[o]).astype(jnp.bfloat16)
        cs[o, :, 0:128] = value[:ROWS, :128]
        cs[o, :, 128:256] = value[ROWS:, :128]
        cs[o, :, 256:384] = value[:ROWS, 128:]
        cs[o, :, 384:512] = value[ROWS:, 128:]
    for o in range(ORI):
        for q in range(2):
            even = dot(cs[o, :, :256], spread[0, :, q * 256 : (q + 1) * 256])
            odd = dot(cs[o, :, 256:], spread[1, :, q * 256 : (q + 1) * 256])
            for h, spec in enumerate((even + odd, even - odd)):
                lanes = slice((2 * h + q) * 128, (2 * h + q + 1) * 128)
                t_re, t_im = folded[:ROWS, lanes], folded[ROWS:, lanes]
                s_re, s_im = spec[:, :128], spec[:, 128:]
                re = t_re * s_re + t_im * s_im
                im = t_im * s_re - t_re * s_im
                prod[o, q, 8:, h * 128 : (h + 1) * 128] = re[8:BOX].astype(jnp.bfloat16)
                prod[o, q, 8:, 256 + h * 128 : 256 + (h + 1) * 128] = im[8:BOX].astype(jnp.bfloat16)
                top_re = re[:8] - im[BOX : BOX + 8]
                top_im = im[:8] + re[BOX : BOX + 8]
                prod[o, q, :8, h * 128 : (h + 1) * 128] = top_re.astype(jnp.bfloat16)
                prod[o, q, :8, 256 + h * 128 : 256 + (h + 1) * 128] = top_im.astype(jnp.bfloat16)
    for o in range(ORI):
        even = dot(prod[o, 0], inverse[0])
        odd = dot(prod[o, 1], inverse[1])
        low, high = (even + odd).astype(jnp.bfloat16), (even - odd).astype(jnp.bfloat16)
        for parity in range(2):
            rows = slice(parity * 128, (parity + 1) * 128)
            half[o, parity, :128, :256] = low[rows, :256]
            half[o, parity, 128:, :256] = low[rows, 256:]
            half[o, parity, :128, 256:] = high[rows, :256]
            half[o, parity, 128:, 256:] = high[rows, 256:]
    outs = []
    for block in range(2):
        lanes = slice(block * 256, (block + 1) * 256)
        for o in range(ORI):
            even_part[o] = dot(final[0], half[o, 0, :, lanes])
            odd_part[o] = dot(final[1], half[o, 1, :, lanes])

        def combine(i, carry):
            rows = pl.ds(pl.multiple_of(i * 16, 16), 16)
            high_rows = pl.ds(pl.multiple_of(i * 16 + BOX, 16), 16)
            for sign, dest in ((1, rows), (-1, high_rows)):
                peak, run, energy = max_ref[0, dest, lanes], sum_ref[0, dest, lanes], sumsq_ref[0, dest, lanes]
                for o in range(ORI):
                    even, odd = even_part[o, rows, :], odd_part[o, rows, :]
                    score = even + odd if sign == 1 else even - odd
                    peak, run, energy = jnp.maximum(peak, score), run + score, energy + score * score
                best[dest, lanes], total[dest, lanes], square[dest, lanes] = peak, run, energy
            return carry

        lax.fori_loop(0, BOX // 16, combine, 0)
        for i, (src, dst) in enumerate(((best, out_max_ref), (total, out_sum_ref), (square, out_sumsq_ref))):
            copy = pltpu.make_async_copy(src.at[:, lanes], dst.at[0, :, lanes], out_sem.at[block * 3 + i])
            copy.start()
            outs.append(copy)
    for copy in outs:
        copy.wait()


def body(map_slabs, slot_slab, orient_index, slab_lo, slab_hi, tile_spectrum, prev_max, prev_sum, prev_sumsq):
    column, spread, inverse, final = (jnp.asarray(t) for t in tables())
    smem = pl.BlockSpec(memory_space=pltpu.SMEM)
    hbm = pl.BlockSpec(memory_space=pl.ANY)
    vmem = pltpu.VMEM
    in_hbm = lambda a: pltpu.with_memory_space_constraint(a, pltpu.HBM)
    template, folded = pl.pallas_call(
        project_kernel,
        name="project",
        out_shape=(
            vmem((ORI, BOX, BOX), jnp.bfloat16),
            vmem((2 * ROWS, TILE), jnp.float32),
        ),
        in_specs=[smem] * 4 + [hbm] * 2,
        out_specs=(pl.BlockSpec(memory_space=vmem),) * 2,
        scratch_shapes=[
            vmem((SLOTS, SLAB_Z, BOX, BOX), jnp.bfloat16),
            vmem((TILE, 2 * TILE), jnp.bfloat16),
            vmem((2 * ROWS, TILE), jnp.bfloat16),
            vmem((2 * TILE, TILE), jnp.bfloat16),
            vmem((SLAB_Z, BOX, BOX), jnp.bfloat16),
            vmem((SLAB_Z * BOX, BOX), jnp.bfloat16),
            vmem((BOX, SLAB_Z * BOX), jnp.bfloat16),
            vmem((BOX, BOX), jnp.float32),
            vmem((HALF, BOX), jnp.float32),
            vmem((HALF, BOX), jnp.bfloat16),
            vmem((HALF, BOX), jnp.bfloat16),
            vmem((2 * ROWS, 2 * TILE), jnp.bfloat16),
            pltpu.SemaphoreType.DMA((1,)),
            pltpu.SemaphoreType.DMA((SLOTS,)),
            pltpu.SemaphoreType.DMA((9,)),
            pltpu.SemaphoreType.DMA((9,)),
        ],
        compiler_params=pltpu.CompilerParams(
            collective_id=0, has_side_effects=True, vmem_limit_bytes=50 << 20
        ),
    )(*(in_hbm(a) for a in (orient_index, slot_slab, slab_lo, slab_hi)), in_hbm(map_slabs), in_hbm(tile_spectrum))
    plane = jax.ShapeDtypeStruct((1, TILE, TILE), jnp.float32)
    return pl.pallas_call(
        correlate_kernel,
        name="correlate",
        out_shape=(plane, plane, plane),
        in_specs=[pl.BlockSpec(memory_space=vmem)] * 9,
        out_specs=(hbm, hbm, hbm),
        scratch_shapes=[
            vmem((TILE, TILE), jnp.float32),
            vmem((TILE, TILE), jnp.float32),
            vmem((TILE, TILE), jnp.float32),
            vmem((ORI, ROWS, TILE), jnp.bfloat16),
            vmem((ORI, 2, BOX, TILE), jnp.bfloat16),
            vmem((ORI, 2, BOX, TILE), jnp.bfloat16),
            vmem((ORI, BOX, BOX), jnp.float32),
            vmem((ORI, BOX, BOX), jnp.float32),
            pltpu.SemaphoreType.DMA((6,)),
        ],
        compiler_params=pltpu.CompilerParams(vmem_limit_bytes=40 << 20),
    )(template, folded, column, spread, inverse, final, prev_max, prev_sum, prev_sumsq)


def solution(mesh):
    tile_spec = P(("mic", "proj"), None, None)
    return jax.shard_map(
        body,
        mesh=mesh,
        in_specs=(P("proj", None, None, None), P("proj"), P(), P(), P(), tile_spec, tile_spec, tile_spec, tile_spec),
        out_specs=(tile_spec, tile_spec, tile_spec),
        check_vma=False,
    )
```
